512 devices in a mesh: geo: 128 (over y, z, core), deg: 4 (over x).
Axes of the slice: x: 4, y: 8, z: 8, core: 2. Of those that a mesh axis runs over, the one named last changes fastest.
Arguments:
- lo_ainv: bfloat16 [20, 20, 65536], P(None, None, ('geo', 'deg')), may hold values from -1.25 to 1.25
- lo_geom: float32 [12, 65536], P(None, ('geo', 'deg')), may hold values from -1.5 to 1.5
- lo_load: bfloat16 [20, 65536], P(None, ('geo', 'deg')), may hold values from -6 to 6
- lo_degree: int32 [65536], P(('geo', 'deg')), may hold values from 1 to 3, as said below
- lo_send: int32 [4, 65536], P(None, ('geo', 'deg')), may hold values from 0 to 767, as said below
- hi_geom: float32 [12, 65536], P(None, ('geo', 'deg')), may hold values from -1.5 to 1.5
- hi_load: bfloat16 [84, 65536], P(None, ('geo', 'deg')), may hold values from -6 to 6
- hi_degree: int32 [65536], P(('geo', 'deg')), may hold values from 0 to 6, as said below
- hi_slot: int32 [65536], P(('geo', 'deg')), may hold values from -1 to 127, as said below
- hi_ainv: bfloat16 [84, 84, 65536], P(None, None, ('geo', 'deg')), may hold values from -0.625 to 0.625
- hi_send: int32 [4, 65536], P(None, ('geo', 'deg')), may hold values from -1 to 767, as said below
- recv_face: int32 [786432], P(('geo', 'deg')), may hold values from -1 to 767, as said below
- lift_ref: float32 [4, 4, 28, 84], replicated, may hold values from -1.25 to 1.25
- trace_ref: float32 [4, 84, 4, 28], replicated, may hold values from -1.25 to 1.25
- face_mass: float32 [28, 28], replicated, may hold values from -2 to 2
Outputs:
- low_particular: float32 [20, 65536], P(None, ('geo', 'deg'))
- high_particular: float32 [84, 65536], P(None, ('geo', 'deg'))
- trace_blocks: float32 [28, 28, 393216], P(None, None, ('geo', 'deg'))
- trace_rhs: float32 [28, 393216], P(None, ('geo', 'deg'))
The draws below stay inside these ranges and needn't reach their ends.
Inputs may be any that keep to these rules, and one draw needn't show every extreme that they name: `lo_degree`: every LOW position holds an element of degree 1, 2 or 3. `hi_degree`: 0 where the position holds no element, else 4, 5 or 6. `hi_slot`: -1 exactly where hi_degree is 0; the other values are distinct on a device, so at most 32 elements go from one device to one device of its deg group; in some geo index every batch slot is filled. `lo_send`: values are distinct on a device, so at most 6 rows go from one device to one owner; some owners receive 6 LOW rows from every device of their deg index. `hi_send`: -1 exactly for the faces of batch slots that receive no element; the other values are distinct on a device; some owners receive 6 HIGH rows from every device of their deg index. `recv_face`: -1 exactly where no row arrives; a face of a device is named at most twice among that device's entries.
All inputs are finite; a program needn't handle non-finite values.
Results may differ from the reference program's by a relative error of at most 0.0095.
Values may be sent and summed in bfloat16 or wider, within the bound.
A program may use at most 64 MiB of HBM per device.

```python
import jax
import jax.numpy as jnp
from jax import lax

NI_HI = 84
NF_HI = 28
NI_LO = 20
NF_LO = 10
TERMS = 4
E_LO = 128
CAP_R = 32
GEOM = 12
E_HI = 128
CAP_LO = 6
CAP_HI = 6
F_DEV = 768
ELEMS_LO = 65536
ELEMS_HI = 65536
FACES = 393216
N_GEO = 128
N_DEG = 4
DEVICES = 512


def shuffled(seed_key, how_many, length):
    key_list = jax.random.split(seed_key, how_many)
    return jax.vmap(lambda single_key: jax.random.permutation(single_key, length))(key_list)


def place_rows(seed_key, live_rows, capacity, hot_owner):
    slot_total = N_GEO * capacity
    incidences = live_rows.shape[2]
    senders = N_DEG * N_GEO
    first_key = jax.random.fold_in(seed_key, 1)
    second_key = jax.random.fold_in(seed_key, 2)
    slot_rank = shuffled(first_key, senders, slot_total).reshape(N_DEG, N_GEO, slot_total)
    owner_of_slot = jnp.arange(slot_total) // capacity
    hot_slot = hot_owner[:, owner_of_slot]
    slot_score = slot_rank + jnp.where(hot_slot[:, None, :], 0, slot_total)
    slot_order = jnp.argsort(slot_score, axis=2, stable=True)
    row_rank = shuffled(second_key, senders, incidences).reshape(N_DEG, N_GEO, incidences)
    row_score = jnp.where(live_rows, row_rank, incidences + row_rank)
    row_order = jnp.argsort(row_score, axis=2, stable=True)
    live_total = jnp.sum(live_rows.astype(jnp.int32), axis=2, keepdims=True)
    sequence = jnp.arange(incidences)[None, None, :]
    assigned = jnp.where(sequence < live_total, slot_order[:, :, :incidences], -1)
    inverse_order = jnp.argsort(row_order, axis=2, stable=True)
    return jnp.take_along_axis(assigned, inverse_order, axis=2)


def mark_used(positions, slot_total):
    target = jnp.where(positions < 0, slot_total, positions)
    plane_index = jnp.arange(positions.shape[0])[:, None, None]
    sender_index = jnp.arange(positions.shape[1])[None, :, None]
    marks = jnp.zeros((positions.shape[0], positions.shape[1], slot_total + 1), jnp.int32)
    marks = marks.at[plane_index, sender_index, target].set(1)
    return marks[:, :, :slot_total]


def build_layout(base_key):
    level_key = jax.random.fold_in(base_key, 7001)
    group_key = jax.random.fold_in(base_key, 7002)
    pair_key = jax.random.fold_in(base_key, 7003)
    rank_key = jax.random.fold_in(base_key, 7004)
    code_key = jax.random.fold_in(base_key, 7005)
    degree_key = jax.random.fold_in(base_key, 7006)
    low_key = jax.random.fold_in(base_key, 7007)
    hot_key = jax.random.fold_in(base_key, 7008)
    low_place_key = jax.random.fold_in(base_key, 7009)
    high_place_key = jax.random.fold_in(base_key, 7010)
    order_key = jax.random.fold_in(base_key, 7011)
    face_key = jax.random.fold_in(base_key, 7012)
    levels = jax.random.randint(level_key, (N_GEO, N_DEG, N_DEG), CAP_R // 4, CAP_R + 1)
    full_group = jax.random.randint(group_key, (), 0, N_GEO)
    full_pair = jax.random.randint(pair_key, (N_GEO,), 0, N_DEG * N_DEG)
    group_index = jnp.arange(N_GEO)[:, None, None]
    pair_index = (jnp.arange(N_DEG)[:, None] * N_DEG + jnp.arange(N_DEG)[None, :])[None, :, :]
    levels = jnp.where((group_index == full_group) | (pair_index == full_pair[:, None, None]), CAP_R, levels)
    slot_rank = shuffled(rank_key, N_GEO * N_DEG * N_DEG, CAP_R).reshape(N_GEO, N_DEG, N_DEG, CAP_R)
    slot_live = slot_rank < levels[..., None]
    slot_codes = shuffled(code_key, N_GEO * N_DEG, E_HI).reshape(N_GEO, N_DEG, E_HI)
    element_live = jnp.take_along_axis(slot_live.reshape(N_GEO, N_DEG, E_HI), slot_codes, axis=2)
    high_slot = jnp.where(element_live, slot_codes, -1).reshape(-1)
    degrees = jax.random.randint(degree_key, (N_GEO, N_DEG, E_HI), 4, 7)
    high_degree = jnp.where(element_live, degrees, 0).reshape(-1)
    low_degree = jax.random.randint(low_key, (N_GEO * N_DEG * E_LO,), 1, 4)
    batch_live = jnp.transpose(slot_live, (0, 2, 1, 3)).reshape(N_GEO, N_DEG, E_HI)
    hot_rank = shuffled(hot_key, N_DEG, N_GEO)
    hot_owner = hot_rank < max(1, N_GEO // 16)
    low_live = jnp.ones((N_DEG, N_GEO, 4 * E_LO), dtype=bool)
    plane_live = jnp.transpose(batch_live, (1, 0, 2))[:, :, None, :]
    high_live = jnp.broadcast_to(plane_live, (N_DEG, N_GEO, 4, E_HI)).reshape(N_DEG, N_GEO, 4 * E_HI)
    low_place = place_rows(low_place_key, low_live, CAP_LO, hot_owner)
    high_place = place_rows(high_place_key, high_live, CAP_HI, hot_owner)
    low_used = mark_used(low_place, N_GEO * CAP_LO).reshape(N_DEG, N_GEO, N_GEO, CAP_LO)
    high_used = mark_used(high_place, N_GEO * CAP_HI).reshape(N_DEG, N_GEO, N_GEO, CAP_HI)
    received = jnp.concatenate([jnp.transpose(low_used, (0, 2, 1, 3)), jnp.transpose(high_used, (0, 2, 1, 3))], axis=3)
    total_rows = N_GEO * (CAP_LO + CAP_HI)
    received = received.reshape(N_DEG, N_GEO, total_rows) > 0
    order_rank = shuffled(order_key, N_DEG * N_GEO, total_rows).reshape(N_DEG, N_GEO, total_rows)
    order_score = jnp.where(received, order_rank, total_rows + order_rank)
    sorted_rows = jnp.argsort(order_score, axis=2, stable=True)
    row_position = jnp.argsort(sorted_rows, axis=2, stable=True)
    face_perm = shuffled(face_key, N_DEG * N_GEO, F_DEV).reshape(N_DEG, N_GEO, F_DEV)
    face_local = jnp.take_along_axis(face_perm, row_position // 2, axis=2)
    receive_plan = jnp.where(received, face_local, -1)
    receive_plan = jnp.transpose(receive_plan, (1, 0, 2)).reshape(-1)
    low_send = jnp.transpose(low_place.reshape(N_DEG, N_GEO, 4, E_LO), (2, 1, 0, 3)).reshape(4, N_GEO * N_DEG * E_LO)
    high_send = jnp.transpose(high_place.reshape(N_DEG, N_GEO, 4, E_HI), (2, 1, 0, 3)).reshape(4, N_GEO * N_DEG * E_HI)
    return (low_degree.astype(jnp.int32), low_send.astype(jnp.int32), high_degree.astype(jnp.int32), high_slot.astype(jnp.int32), high_send.astype(jnp.int32), receive_plan.astype(jnp.int32))


def draw_lo_degree(key, part):
    return build_layout(key)[0]


def draw_lo_send(key, part):
    return build_layout(key)[1]


def draw_hi_degree(key, part):
    return build_layout(key)[2]


def draw_hi_slot(key, part):
    return build_layout(key)[3]


def draw_hi_send(key, part):
    return build_layout(key)[4]


def draw_recv_face(key, part):
    return build_layout(key)[5]


def shard_levels(rng, shape, shards, smallest, high):
    def one(position, parts):
        steps = jax.random.uniform(jax.random.fold_in(jax.random.fold_in(rng, 6), position), (parts,), jnp.float32, smallest / len(shards), high / len(shards))
        return jnp.repeat(jnp.exp(steps), shape[position] // parts).reshape((-1,) + (1,) * (len(shape) - position - 1))

    factor_of = one(*shards[0])
    for cut in shards[1:]:
        factor_of = factor_of * one(*cut)
    return factor_of


def scatter_about(stream_key, dims, scale, limit, shards=(), kind=jnp.bfloat16):
    values = jax.random.normal(stream_key, dims, jnp.float32) * scale
    if len(shards) > 0:
        values = shard_levels(stream_key, dims, shards, -0.22, 0.18) * values
    return jnp.clip(values, min=-limit, max=limit).astype(kind)


def setup_inputs(seed: int = 0) -> dict:
    streams_of = jax.random.split(jax.random.key(seed), 16)
    lo_ainv = scatter_about(streams_of[0], (NI_LO, NI_LO, ELEMS_LO), NI_LO ** -0.5, 1.25, ((2, 512),))
    lo_geom = jnp.clip(jax.random.uniform(streams_of[1], (GEOM, ELEMS_LO), jnp.float32, -1.5, 1.5) * shard_levels(streams_of[1], (GEOM, ELEMS_LO), ((1, 512),), -0.4, 0.0), -1.5, 1.5)
    lo_load = scatter_about(streams_of[2], (NI_LO, ELEMS_LO), 1.0, 6.0, ((1, 512),))
    lo_degree = draw_lo_degree(jax.random.fold_in(streams_of[15], 71), 0)
    lo_send = draw_lo_send(jax.random.fold_in(streams_of[15], 71), 0)
    hi_geom = jnp.clip(jax.random.uniform(streams_of[5], (GEOM, ELEMS_HI), jnp.float32, -1.5, 1.5) * shard_levels(streams_of[5], (GEOM, ELEMS_HI), ((1, 512),), -0.4, 0.0), -1.5, 1.5)
    hi_load = scatter_about(streams_of[6], (NI_HI, ELEMS_HI), 1.0, 6.0, ((1, 512),))
    hi_degree = draw_hi_degree(jax.random.fold_in(streams_of[15], 71), 0)
    hi_slot = draw_hi_slot(jax.random.fold_in(streams_of[15], 71), 0)
    hi_ainv = scatter_about(streams_of[9], (NI_HI, NI_HI, ELEMS_HI), NI_HI ** -0.5, 0.625, ((2, 512),))
    hi_send = draw_hi_send(jax.random.fold_in(streams_of[15], 71), 0)
    recv_face = draw_recv_face(jax.random.fold_in(streams_of[15], 71), 0)
    lift_ref = scatter_about(streams_of[12], (TERMS, 4, NF_HI, NI_HI), (NI_HI // 4) ** -0.5, 1.25, (), jnp.float32)
    trace_ref = scatter_about(streams_of[13], (TERMS, NI_HI, 4, NF_HI), (NI_HI // 4) ** -0.5, 1.25, (), jnp.float32)
    face_mass = scatter_about(streams_of[14], (NF_HI, NF_HI), (NF_HI // 4) ** -0.5, 2.0, (), jnp.float32)
    return dict(lo_ainv=lo_ainv, lo_geom=lo_geom, lo_load=lo_load, lo_degree=lo_degree, lo_send=lo_send, hi_geom=hi_geom, hi_load=hi_load, hi_degree=hi_degree, hi_slot=hi_slot, hi_ainv=hi_ainv, hi_send=hi_send, recv_face=recv_face, lift_ref=lift_ref, trace_ref=trace_ref, face_mass=face_mass)


def prefix_masks(degree_value, inner_width, face_width):
    inner_count = (degree_value + 1.0) * (degree_value + 2.0) * (degree_value + 3.0) / 6.0
    face_count = (degree_value + 1.0) * (degree_value + 2.0) / 2.0
    inner_mask = (jnp.arange(inner_width, dtype=jnp.float32)[:, None] < inner_count[None, :]).astype(jnp.float32)
    face_mask = (jnp.arange(face_width, dtype=jnp.float32)[:, None] < face_count[None, :]).astype(jnp.float32)
    return inner_mask, face_mask


def condense(inverse, geometry, load_values, degree_value, lift_table, trace_table, mass_table):
    term_count = lift_table.shape[0]
    face_width = mass_table.shape[0]
    element_count = geometry.shape[1]
    inner_mask, face_mask = prefix_masks(degree_value, inverse.shape[0], face_width)
    lift_mix = jnp.einsum("kaij,ke->aije", lift_table, geometry[:term_count], precision=lax.Precision.HIGHEST)
    lift_mat = (lift_mix * face_mask[None, :, None, :] * inner_mask[None, None, :, :]).astype(jnp.bfloat16)
    trace_mix = jnp.einsum("kjai,ke->jaie", trace_table, geometry[term_count:2 * term_count], precision=lax.Precision.HIGHEST)
    trace_mat = (trace_mix * inner_mask[:, None, None, :] * face_mask[None, None, :, :]).astype(jnp.bfloat16)
    solved = jnp.einsum("jle,laie->jaie", inverse.astype(jnp.float32), trace_mat.astype(jnp.float32), precision=lax.Precision.HIGHEST).astype(jnp.bfloat16)
    coupling = jnp.einsum("aije,jame->imae", lift_mat.astype(jnp.float32), solved.astype(jnp.float32), precision=lax.Precision.HIGHEST)
    scaling = geometry[2 * term_count:2 * term_count + 4]
    pair_mask = face_mask[:, None, :] * face_mask[None, :, :]
    schur_block = mass_table[:, :, None, None] * scaling[None, None, :, :] * pair_mask[:, :, None, :] - coupling
    masked_load = load_values * inner_mask.astype(jnp.bfloat16)
    particular = inner_mask * jnp.einsum("jle,le->je", inverse.astype(jnp.float32), masked_load.astype(jnp.float32), precision=lax.Precision.HIGHEST)
    rounded_part = particular.astype(jnp.bfloat16).astype(jnp.float32)
    rhs_part = -jnp.einsum("aije,je->iae", lift_mat.astype(jnp.float32), rounded_part, precision=lax.Precision.HIGHEST)
    face_rows = jnp.concatenate([schur_block.reshape(face_width * face_width, 4 * element_count), rhs_part.reshape(face_width, 4 * element_count)], axis=0)
    return face_rows.astype(jnp.bfloat16), particular


def take_block(array, device, width):
    start = (device * width).astype(jnp.int32)
    return lax.dynamic_slice_in_dim(array, start, width, axis=array.ndim - 1)


def add_rows(blocks, right_side, face_rows, target, narrow):
    values = face_rows.astype(jnp.float32)
    block_part = values[:narrow * narrow].reshape(narrow, narrow, values.shape[1])
    blocks = blocks.at[:narrow, :narrow, target].add(block_part, mode="drop")
    right_side = right_side.at[:narrow, target].add(values[narrow * narrow:], mode="drop")
    return blocks, right_side


def reference(lo_ainv, lo_geom, lo_load, lo_degree, lo_send, hi_geom, hi_load, hi_degree, hi_slot, hi_ainv, hi_send, recv_face, lift_ref, trace_ref, face_mass):
    per_owner = CAP_LO + CAP_HI
    record = jnp.concatenate([hi_geom, hi_load.astype(jnp.float32), hi_degree.astype(jnp.float32)[None, :]], axis=0)
    slot_code = hi_slot.reshape(N_GEO, N_DEG, E_HI)
    target_plane = slot_code // CAP_R
    within_slot = slot_code % CAP_R
    group_index = jnp.arange(N_GEO, dtype=jnp.int32)[:, None, None]
    source_plane = jnp.arange(N_DEG, dtype=jnp.int32)[None, :, None]
    batch_index = ((group_index * N_DEG + target_plane) * N_DEG + source_plane) * CAP_R + within_slot
    batch_index = jnp.where(slot_code < 0, ELEMS_HI, batch_index).reshape(-1).astype(jnp.int32)
    batch_record = jnp.zeros((record.shape[0], ELEMS_HI), jnp.float32).at[:, batch_index].set(record, mode="drop")
    geo_rows = GEOM

    def face_ids(positions, capacity, offset, device):
        group = device // N_DEG
        plane = device % N_DEG
        owner = (positions // capacity) * N_DEG + plane
        flat = (owner * N_GEO + group) * per_owner + offset + positions % capacity
        local = recv_face[jnp.where(positions < 0, 0, flat).astype(jnp.int32)]
        return jnp.where((positions < 0) | (local < 0), FACES, owner * F_DEV + local).astype(jnp.int32)

    def step(carry, device):
        blocks, right_side = carry
        low_rows, low_part = condense(take_block(lo_ainv, device, E_LO), take_block(lo_geom, device, E_LO), take_block(lo_load, device, E_LO), take_block(lo_degree, device, E_LO).astype(jnp.float32), lift_ref[:, :, :NF_LO, :NI_LO], trace_ref[:, :NI_LO, :, :NF_LO], face_mass[:NF_LO, :NF_LO])
        high_record = take_block(batch_record, device, E_HI)
        high_rows, high_part = condense(take_block(hi_ainv, device, E_HI), high_record[:geo_rows], high_record[geo_rows:geo_rows + NI_HI].astype(jnp.bfloat16), high_record[geo_rows + NI_HI], lift_ref, trace_ref, face_mass)
        low_target = face_ids(take_block(lo_send, device, E_LO).reshape(-1), CAP_LO, 0, device)
        high_target = face_ids(take_block(hi_send, device, E_HI).reshape(-1), CAP_HI, CAP_LO, device)
        blocks, right_side = add_rows(blocks, right_side, low_rows, low_target, NF_LO)
        blocks, right_side = add_rows(blocks, right_side, high_rows, high_target, NF_HI)
        return (blocks, right_side), (low_part, high_part)

    start_blocks = jnp.zeros((NF_HI, NF_HI, FACES), jnp.float32)
    start_right = jnp.zeros((NF_HI, FACES), jnp.float32)
    devices_list = jnp.arange(DEVICES, dtype=jnp.int32)
    (trace_blocks, trace_rhs), (low_parts, high_parts) = lax.scan(step, (start_blocks, start_right), devices_list)
    low_particular = jnp.moveaxis(low_parts, 0, 1).reshape(NI_LO, ELEMS_LO)
    high_particular = jnp.moveaxis(high_parts, 0, 1).reshape(NI_HI, ELEMS_HI)
    return (low_particular, high_particular, trace_blocks, trace_rhs)
```

```python
import functools

import jax
import jax.numpy as jnp
from jax import lax
from jax.experimental import pallas as pl
from jax.experimental.pallas import tpu as pltpu
from jax.sharding import PartitionSpec as P

F32 = jnp.float32
BF16 = jnp.bfloat16
LANES = 128
TERMS = 4
NF_LO = 10
NI_LO = 20
LO_PAD = 16
LO_STRIDE = 12
HI_PAD = 32
HI_STRIDE = 32
NT = (((1,), (1,)), ((), ()))
TN = (((0,), (0,)), ((), ()))
VMEM = pl.BlockSpec(memory_space=pltpu.VMEM)


def masks(degree, inner_width, face_width):
    inner_count = (degree + 1.0) * (degree + 2.0) * (degree + 3.0) / 6.0
    face_count = (degree + 1.0) * (degree + 2.0) / 2.0
    elements = degree.shape[1]
    inner_row = lax.broadcasted_iota(jnp.int32, (inner_width, elements), 0).astype(F32)
    face_row = lax.broadcasted_iota(jnp.int32, (face_width, elements), 0).astype(F32)
    inner_mask = (inner_row < inner_count).astype(F32)
    face_mask = (face_row < face_count).astype(F32)
    return inner_mask, face_mask


def condense_body(
    ainv_ref, geom, load, degree, lift_ref, trace_ref, mass_ref, part_ref,
    lmat, solved, masked, rhs_load, stack, massb, width, inner, pad, stride, rows
):
    am = 4 * width
    inner_mask, face_mask = masks(degree, inner, pad)
    masked[...] = inner_mask
    rhs_load[...] = load * inner_mask
    for t in range(TERMS):
        for a in range(4):
            piece = lift_ref[t, a][:width, :inner]
            piece = jnp.concatenate([piece, jnp.zeros((pad - width, inner), F32)], axis=0)
            lmat[a, t * pad:(t + 1) * pad, :] = piece.astype(BF16)
    mass = mass_ref[...][:width, :width]
    mass = jnp.concatenate([mass, jnp.zeros((pad - width, width), F32)], axis=0)
    for m in range(width):
        massb[m] = jnp.broadcast_to(mass[:, m:m + 1], (pad, LANES))
    trace_g = [geom[TERMS + t:TERMS + t + 1, :] for t in range(TERMS)]

    def solve(pair, carry):
        blocks = []
        rows_mask = []
        for k in range(2):
            j = 2 * pair + k
            block = ainv_ref[j].astype(F32)
            row_mask = masked[pl.ds(j, 1), :]
            part_ref[pl.ds(j, 1), :] = row_mask * jnp.sum(block * rhs_load[...], axis=0, keepdims=True)
            blocks.append((block * masked[...]).astype(BF16))
            rows_mask.append(row_mask)
        out = jnp.dot(trace_ref[...], jnp.concatenate(blocks, axis=1), preferred_element_type=F32)
        for k in range(2):
            j = 2 * pair + k
            total = None
            for t in range(TERMS):
                term = out[t * am:(t + 1) * am, k * LANES:(k + 1) * LANES] * (trace_g[t] * rows_mask[k])
                total = term if total is None else total + term
            solved[pl.ds(pl.multiple_of(j * am, 8), am), :] = total
        return carry

    lax.fori_loop(0, inner // 2, solve, 0)

    lift_g = [geom[t:t + 1, :] for t in range(TERMS)]

    def mixed(out, k):
        total = None
        for t in range(TERMS):
            term = out[t * pad:(t + 1) * pad, k * LANES:(k + 1) * LANES] * lift_g[t]
            total = term if total is None else total + term
        return total

    part = part_ref[...].astype(BF16)
    for a in range(4):
        out = jnp.dot(lmat[a], part, preferred_element_type=F32)
        value = -(mixed(out, 0) * face_mask)
        stack[pl.ds(a * rows + width, width, stride=stride), :] = value[:width]
    scales = [geom[2 * TERMS + a:2 * TERMS + a + 1, :] for a in range(4)]

    def couple(pair, carry):
        for a in range(4):
            columns = []
            for k in range(2):
                m = 2 * pair + k
                columns.append(solved[pl.ds(a * width + m, inner, stride=am), :].astype(BF16))
            out = jnp.dot(lmat[a], jnp.concatenate(columns, axis=1), preferred_element_type=F32)
            for k in range(2):
                m = 2 * pair + k
                column_mask = (m.astype(F32) < (degree + 1.0) * (degree + 2.0) / 2.0).astype(F32)
                value = (massb[m] * scales[a] - mixed(out, k)) * (face_mask * column_mask)
                stack[pl.ds(a * rows + m, width, stride=stride), :] = value[:width]
        return carry

    lax.fori_loop(0, width // 2, couple, 0)


def one_hots(send_ref, chosen, capacity):
    groups = chosen.shape[0] // capacity
    for a in range(4):
        positions = send_ref[a:a + 1, :]
        for c in range(capacity):
            want = lax.broadcasted_iota(jnp.int32, (groups, LANES), 0) * capacity + c
            chosen[c * groups:(c + 1) * groups, a * LANES:(a + 1) * LANES] = (
                (want == positions).astype(F32).astype(BF16)
            )


def record_kernel(geom_ref, load_ref, degree_ref, slot_ref, out_ref):
    count = geom_ref.shape[0] + load_ref.shape[0] + 1
    record = jnp.concatenate(
        [load_ref[...].astype(F32), geom_ref[...], degree_ref[...].astype(F32),
         jnp.zeros((LANES - count, LANES), F32)], axis=0
    )
    hot = (lax.broadcasted_iota(jnp.int32, (LANES, LANES), 0) == slot_ref[...]).astype(F32)
    out_ref[...] = lax.dot_general(hot, record, NT, precision=lax.Precision.HIGHEST, preferred_element_type=F32)


def low_kernel(
    capacity, ainv_ref, geom_ref, load_ref, degree_ref, send_ref, lift_ref, trace_ref, mass_ref,
    part_ref, placed_ref, lmat, solved, masked, rhs_load, stack, massb, chosen, rowsb
):
    stack[...] = jnp.zeros_like(stack)
    condense_body(
        ainv_ref, geom_ref[...], load_ref[...].astype(F32), degree_ref[...].astype(F32), lift_ref, trace_ref,
        mass_ref, part_ref, lmat, solved, masked, rhs_load, stack, massb,
        NF_LO, NI_LO, LO_PAD, LO_STRIDE, LANES,
    )
    one_hots(send_ref, chosen, capacity)
    for a in range(4):
        rowsb[:, a * LANES:(a + 1) * LANES] = stack[a * LANES:(a + 1) * LANES, :].astype(BF16)
    placed_ref[...] = lax.dot_general(chosen[...], rowsb[...], NT, preferred_element_type=F32)


def high_kernel(
    capacity, ainv_ref, record_ref, send_ref, lift_ref, trace_ref, mass_ref, low_ref,
    part_ref, out_ref, lmat, solved, masked, rhs_load, stack, massb, chosen, rowsb, rec, wide
):
    inner = ainv_ref.shape[0]
    width = mass_ref.shape[0]
    tiles = width * HI_STRIDE // LANES
    groups = out_ref.shape[0]
    per = out_ref.shape[1]
    rec[...] = record_ref[...].T
    geom = rec[inner:inner + 12, :]
    degree = rec[inner + 12:inner + 13, :]
    stack[...] = jnp.zeros_like(stack)
    condense_body(
        ainv_ref, geom, rec[:inner, :], degree, lift_ref, trace_ref, mass_ref, part_ref,
        lmat, solved, masked, rhs_load, stack, massb,
        width, inner, HI_PAD, HI_STRIDE, width * HI_STRIDE,
    )
    one_hots(send_ref, chosen, capacity)
    rows = width * HI_STRIDE
    for c in range(capacity):
        wide[pl.ds(c * (tiles + 1) + tiles, groups, stride=per), :] = low_ref[c * groups:(c + 1) * groups, :]

    def place(q, carry):
        for a in range(4):
            piece = stack[pl.ds(pl.multiple_of(a * rows + q * LANES, LANES), LANES), :]
            rowsb[:, a * LANES:(a + 1) * LANES] = piece.astype(BF16)
        got = lax.dot_general(chosen[...], rowsb[...], NT, preferred_element_type=F32)
        for c in range(capacity):
            wide[pl.ds(c * (tiles + 1) + q, groups, stride=per), :] = got[c * groups:(c + 1) * groups, :]
        return carry

    lax.fori_loop(0, tiles, place, 0)

    def narrow(o, carry):
        out_ref[o] = wide[pl.ds(pl.multiple_of(o * per, 8), per), :].astype(BF16)
        return carry

    lax.fori_loop(0, groups, narrow, 0)


def accumulate_kernel(capacity, rows_ref, recv_ref, blocks_ref, rhs_ref, wide, hot_lo, hot_hi, low_sum, rhs_sum):
    q = pl.program_id(0)
    groups, per, _ = rows_ref.shape
    faces = blocks_ref.shape[2]
    tiles = per // capacity - 1
    width = blocks_ref.shape[1]
    per_tile = LANES // HI_STRIDE

    def gathered(at):
        pieces = [
            wide[pl.ds(c * (tiles + 1) + at, groups, stride=per), :].astype(BF16) for c in range(capacity)
        ]
        return jnp.concatenate(pieces, axis=0)

    @pl.when(q == 0)
    def _():
        def widen(g, carry):
            wide[pl.ds(pl.multiple_of(g * per, 8), per), :] = rows_ref[g].astype(F32)
            return carry

        lax.fori_loop(0, groups, widen, 0)
        columns = lax.broadcasted_iota(jnp.int32, (groups, faces), 1)
        for c in range(capacity):
            hot_lo[c * groups:(c + 1) * groups, :] = (recv_ref[:, c:c + 1] == columns).astype(F32).astype(BF16)
            hot_hi[c * groups:(c + 1) * groups, :] = (
                (recv_ref[:, capacity + c:capacity + c + 1] == columns).astype(F32).astype(BF16)
            )
        low_sum[...] = lax.dot_general(gathered(tiles), hot_lo[...], TN, preferred_element_type=F32)

    total = lax.dot_general(gathered(q), hot_hi[...], TN, preferred_element_type=F32)
    for k in range(per_tile):
        blocks_ref[k] = total[k * HI_STRIDE:k * HI_STRIDE + width, :]
        rhs_ref[k] = total[k * HI_STRIDE + width:k * HI_STRIDE + width + 1, :]
    for s in range(-(-NF_LO // per_tile)):
        @pl.when(q == s)
        def _():
            for k in range(per_tile):
                i = s * per_tile + k
                if i < NF_LO:
                    low = low_sum[i * LO_STRIDE:i * LO_STRIDE + NF_LO + 1, :]
                    blocks_ref[k, :NF_LO, :] = blocks_ref[k, :NF_LO, :] + low[:NF_LO]
                    rhs_ref[k] = rhs_ref[k] + low[NF_LO:NF_LO + 1]


def on_device(
    lo_ainv, lo_geom, lo_load, lo_degree, lo_send, hi_geom, hi_load, hi_degree, hi_slot, hi_ainv, hi_send,
    recv_face, lift_ref, trace_ref, face_mass,
):
    width = face_mass.shape[0]
    inner, _, elements = hi_ainv.shape
    groups = lax.axis_size("geo")
    capacity = 6 * lo_ainv.shape[2] // groups
    tiles = width * HI_STRIDE // LANES
    per = capacity * (tiles + 1)
    rows = width * HI_STRIDE
    faces = groups * capacity

    record = pl.pallas_call(
        record_kernel,
        out_shape=jax.ShapeDtypeStruct((elements, LANES), F32),
        in_specs=[VMEM] * 4,
        out_specs=VMEM,
        name="record",
    )(hi_geom, hi_load, hi_degree[None, :], hi_slot[None, :])
    record = lax.all_to_all(record, "deg", split_axis=0, concat_axis=0, tiled=True)

    turned = jnp.transpose(trace_ref, (0, 2, 3, 1))
    trace_hi = turned.reshape(TERMS * 4 * width, inner).astype(BF16)
    trace_lo = turned[:, :, :NF_LO, :NI_LO].reshape(TERMS * 4 * NF_LO, NI_LO).astype(BF16)

    low_particular, placed = pl.pallas_call(
        functools.partial(low_kernel, capacity),
        out_shape=(
            jax.ShapeDtypeStruct((NI_LO, elements), F32),
            jax.ShapeDtypeStruct((groups * capacity, LANES), F32),
        ),
        in_specs=[VMEM] * 8,
        out_specs=(VMEM, VMEM),
        scratch_shapes=[
            pltpu.VMEM((4, TERMS * LO_PAD, NI_LO), BF16),
            pltpu.VMEM((NI_LO * 4 * NF_LO, LANES), F32),
            pltpu.VMEM((NI_LO, LANES), F32),
            pltpu.VMEM((NI_LO, LANES), F32),
            pltpu.VMEM((4 * LANES, LANES), F32),
            pltpu.VMEM((NF_LO, LO_PAD, LANES), F32),
            pltpu.VMEM((groups * capacity, 4 * LANES), BF16),
            pltpu.VMEM((LANES, 4 * LANES), BF16),
        ],
        cost_estimate=pl.CostEstimate(flops=400_000_000, bytes_accessed=2_000_000, transcendentals=0),
        name="low",
    )(lo_ainv, lo_geom, lo_load, lo_degree[None, :], lo_send, lift_ref, trace_lo, face_mass)

    high_particular, outgoing = pl.pallas_call(
        functools.partial(high_kernel, capacity),
        out_shape=(
            jax.ShapeDtypeStruct((inner, elements), F32),
            jax.ShapeDtypeStruct((groups, per, LANES), BF16),
        ),
        in_specs=[VMEM] * 7,
        out_specs=(VMEM, VMEM),
        scratch_shapes=[
            pltpu.VMEM((4, TERMS * HI_PAD, inner), BF16),
            pltpu.VMEM((inner * 4 * width, LANES), F32),
            pltpu.VMEM((inner, LANES), F32),
            pltpu.VMEM((inner, LANES), F32),
            pltpu.VMEM((4 * rows, LANES), F32),
            pltpu.VMEM((width, HI_PAD, LANES), F32),
            pltpu.VMEM((groups * capacity, 4 * LANES), BF16),
            pltpu.VMEM((LANES, 4 * LANES), BF16),
            pltpu.VMEM((LANES, LANES), F32),
            pltpu.VMEM((groups * per, LANES), F32),
        ],
        compiler_params=pltpu.CompilerParams(vmem_limit_bytes=48 << 20),
        name="high",
    )(hi_ainv, record, hi_send, lift_ref, trace_hi, face_mass, placed)

    arrived = lax.all_to_all(outgoing, "geo", split_axis=0, concat_axis=0, tiled=True)

    plan = recv_face.reshape(groups, 2 * capacity)
    per_tile = LANES // HI_STRIDE
    blocks, right = pl.pallas_call(
        functools.partial(accumulate_kernel, capacity),
        out_shape=(
            jax.ShapeDtypeStruct((width, width, faces), F32),
            jax.ShapeDtypeStruct((width, 1, faces), F32),
        ),
        grid=(tiles,),
        in_specs=[
            pl.BlockSpec((groups, per, LANES), lambda q: (0, 0, 0)),
            pl.BlockSpec((groups, 2 * capacity), lambda q: (0, 0)),
        ],
        out_specs=(
            pl.BlockSpec((per_tile, width, faces), lambda q: (q, 0, 0)),
            pl.BlockSpec((per_tile, 1, faces), lambda q: (q, 0, 0)),
        ),
        scratch_shapes=[
            pltpu.VMEM((groups * per, LANES), F32),
            pltpu.VMEM((groups * capacity, faces), BF16),
            pltpu.VMEM((groups * capacity, faces), BF16),
            pltpu.VMEM((LANES, faces), F32),
            pltpu.VMEM((8, LANES), F32),
        ],
        compiler_params=pltpu.CompilerParams(vmem_limit_bytes=48 << 20),
        name="accumulate",
    )(arrived, plan)
    return (low_particular, high_particular, blocks, right.reshape(width, faces))


def solution(mesh):
    both = ("geo", "deg")
    in_specs = (
        P(None, None, both), P(None, both), P(None, both), P(both), P(None, both), P(None, both), P(None, both),
        P(both), P(both), P(None, None, both), P(None, both), P(both), P(), P(), P(),
    )
    out_specs = (P(None, both), P(None, both), P(None, None, both), P(None, both))
    return jax.shard_map(on_device, mesh=mesh, in_specs=in_specs, out_specs=out_specs, check_vma=False)
```

```python
import functools

import jax
import jax.numpy as jnp
from jax import lax
from jax.experimental import pallas as pl
from jax.experimental.pallas import tpu as pltpu
from jax.sharding import PartitionSpec as P

F32 = jnp.float32
BF16 = jnp.bfloat16
LANES = 128
TERMS = 4
NF_LO = 10
NI_LO = 20
LO_PAD = 16
HI_PAD = 32
SKEW = 4
UNROLL = 2
UNROLL_C = 1
NT = (((1,), (1,)), ((), ()))
TN = (((0,), (0,)), ((), ()))
VMEM = pl.BlockSpec(memory_space=pltpu.VMEM)


def masks(degree, inner_width, face_width):
    inner_count = (degree + 1.0) * (degree + 2.0) * (degree + 3.0) / 6.0
    face_count = (degree + 1.0) * (degree + 2.0) / 2.0
    elements = degree.shape[1]
    inner_row = lax.broadcasted_iota(jnp.int32, (inner_width, elements), 0).astype(F32)
    face_row = lax.broadcasted_iota(jnp.int32, (face_width, elements), 0).astype(F32)
    inner_mask = (inner_row < inner_count).astype(F32)
    face_mask = (face_row < face_count).astype(F32)
    return inner_mask, face_mask


def condense_body(
    ainv_ref, geom, load, degree, lift_ref, trace_ref, mass_ref, part_ref,
    lmat, solved, masked, rhs_load, stack, massb, width, inner, pad, rows
):
    am = 4 * width
    depth = trace_ref.shape[1] // TERMS
    inner_mask, face_mask = masks(degree, inner, pad)
    masked[...] = inner_mask
    rhs_load[...] = load * inner_mask
    for t in range(TERMS):
        for a in range(4):
            piece = lift_ref[t, a][:width, :inner]
            piece = jnp.concatenate([piece, jnp.zeros((pad - width, inner), F32)], axis=0)
            for g in range(pad // 8):
                at = (g * TERMS + t) * 8
                lmat[a, at:at + 8, :] = piece[g * 8:(g + 1) * 8].astype(BF16)
    mass = mass_ref[...][:width, :width]
    mass = jnp.concatenate([mass, jnp.zeros((pad - width, width), F32)], axis=0)
    for m in range(width):
        massb[m] = jnp.broadcast_to(mass[:, m:m + 1], (pad, LANES))

    def combined(out, k, g, scales):
        total = None
        for t in range(TERMS):
            at = (g * TERMS + t) * 8
            term = out[at:at + 8, k * LANES:(k + 1) * LANES] * scales[t]
            total = term if total is None else total + term
        return total

    trace_g = [geom[TERMS + t:TERMS + t + 1, :] for t in range(TERMS)]

    filler = jnp.zeros((depth - inner, LANES), F32)

    def solve(pair, carry):
        columns = []
        for k in range(2):
            j = 2 * pair + k
            block = ainv_ref[j].astype(F32)
            row_mask = masked[pl.ds(j, 1), :]
            part_ref[pl.ds(j, 1), :] = row_mask * jnp.sum(block * rhs_load[...], axis=0, keepdims=True)
            block = block * masked[...]
            stacked = []
            for t in range(TERMS):
                stacked += [block * (trace_g[t] * row_mask), filler]
            columns.append(jnp.concatenate(stacked, axis=0).astype(BF16))
        out = jnp.dot(trace_ref[...], jnp.concatenate(columns, axis=1), preferred_element_type=F32)
        for k in range(2):
            solved[pl.ds(2 * pair + k, am, stride=inner), :] = out[:, k * LANES:(k + 1) * LANES]
        return carry

    lax.fori_loop(0, inner // 2, solve, 0, unroll=UNROLL)

    lift_g = [jnp.broadcast_to(geom[t:t + 1, :], (8, LANES)) for t in range(TERMS)]

    def mixed(out, k):
        return jnp.concatenate([combined(out, k, g, lift_g) for g in range(pad // 8)], axis=0)

    part = part_ref[...].astype(BF16)
    for a in range(4):
        out = jnp.dot(lmat[a], part, preferred_element_type=F32)
        value = -(mixed(out, 0) * face_mask)
        stack[a * rows + width * width:a * rows + width * width + width, :] = value[:width]
    scales = [geom[2 * TERMS + a:2 * TERMS + a + 1, :] for a in range(4)]

    def couple(pair, carry):
        for a in range(4):
            columns = []
            for k in range(2):
                m = 2 * pair + k
                columns.append(solved[pl.ds((a * width + m) * inner, inner), :].astype(BF16))
            out = jnp.dot(lmat[a], jnp.concatenate(columns, axis=1), preferred_element_type=F32)
            for k in range(2):
                m = 2 * pair + k
                column_mask = (m.astype(F32) < (degree + 1.0) * (degree + 2.0) / 2.0).astype(F32)
                value = (massb[m] * scales[a] - mixed(out, k)) * (face_mask * column_mask)
                stack[pl.ds(a * rows + m * width, width), :] = value[:width]
        return carry

    lax.fori_loop(0, width // 2, couple, 0, unroll=UNROLL_C)


def one_hots(send_ref, chosen, capacity):
    groups = chosen.shape[0] // capacity
    for a in range(4):
        positions = send_ref[a:a + 1, :]
        for c in range(capacity):
            want = lax.broadcasted_iota(jnp.int32, (groups, LANES), 0) * capacity + c
            chosen[c * groups:(c + 1) * groups, a * LANES:(a + 1) * LANES] = (
                (want == positions).astype(F32).astype(BF16)
            )


def record_kernel(geom_ref, load_ref, degree_ref, slot_ref, out_ref):
    count = geom_ref.shape[0] + load_ref.shape[0] + 1
    record = jnp.concatenate(
        [load_ref[...].astype(F32), geom_ref[...], degree_ref[...].astype(F32),
         jnp.zeros((LANES - count, LANES), F32)], axis=0
    )
    hot = (lax.broadcasted_iota(jnp.int32, (LANES, LANES), 0) == slot_ref[...]).astype(F32)
    out_ref[...] = lax.dot_general(hot, record, NT, precision=lax.Precision.HIGHEST, preferred_element_type=F32)


def low_kernel(
    capacity, ainv_ref, geom_ref, load_ref, degree_ref, send_ref, lift_ref, trace_ref, mass_ref,
    part_ref, placed_ref, lmat, solved, masked, rhs_load, stack, massb, chosen, rowsb
):
    stack[...] = jnp.zeros_like(stack)
    condense_body(
        ainv_ref, geom_ref[...], load_ref[...].astype(F32), degree_ref[...].astype(F32), lift_ref, trace_ref,
        mass_ref, part_ref, lmat, solved, masked, rhs_load, stack, massb,
        NF_LO, NI_LO, LO_PAD, LANES,
    )
    one_hots(send_ref, chosen, capacity)
    for a in range(4):
        rowsb[:, a * LANES:(a + 1) * LANES] = stack[a * LANES:(a + 1) * LANES, :].astype(BF16)
    placed_ref[...] = lax.dot_general(chosen[...], rowsb[...], NT, preferred_element_type=F32)


def high_kernel(
    capacity, ainv_ref, record_ref, send_ref, lift_ref, trace_ref, mass_ref, low_ref,
    part_ref, out_ref, lmat, solved, masked, rhs_load, stack, massb, chosen, rowsb, rec, wide
):
    inner = ainv_ref.shape[0]
    width = mass_ref.shape[0]
    groups = out_ref.shape[0]
    per = out_ref.shape[1]
    tiles = per // capacity - 1
    rows = tiles * LANES
    step = per + SKEW
    rec[...] = record_ref[...].T
    geom = rec[inner:inner + 12, :]
    degree = rec[inner + 12:inner + 13, :]
    used = width * (width + 1)
    for a in range(4):
        stack[a * rows + used:(a + 1) * rows, :] = jnp.zeros((rows - used, LANES), F32)
    condense_body(
        ainv_ref, geom, rec[:inner, :], degree, lift_ref, trace_ref, mass_ref, part_ref,
        lmat, solved, masked, rhs_load, stack, massb,
        width, inner, HI_PAD, rows,
    )
    one_hots(send_ref, chosen, capacity)
    for c in range(capacity):
        wide[pl.ds(tiles * capacity + c, groups, stride=step), :] = low_ref[c * groups:(c + 1) * groups, :]

    def place(q, count):
        for k in range(count):
            for a in range(4):
                piece = stack[pl.ds(pl.multiple_of(a * rows + (q + k) * LANES, LANES), LANES), :]
                rowsb[k * LANES:(k + 1) * LANES, a * LANES:(a + 1) * LANES] = piece.astype(BF16)
        got = lax.dot_general(chosen[...], rowsb[:count * LANES], NT, preferred_element_type=F32)
        for k in range(count):
            for c in range(capacity):
                wide[pl.ds((q + k) * capacity + c, groups, stride=step), :] = (
                    got[c * groups:(c + 1) * groups, k * LANES:(k + 1) * LANES]
                )

    def place_pair(pair, carry):
        place(2 * pair, 2)
        return carry

    lax.fori_loop(0, tiles // 2, place_pair, 0)
    if tiles % 2:
        place(tiles - 1, 1)

    def narrow(o, carry):
        out_ref[o] = wide[pl.ds(o * step, per), :].astype(BF16)
        return carry

    lax.fori_loop(0, groups, narrow, 0, unroll=4)


def accumulate_kernel(capacity, width, rows_ref, recv_ref, blocks_ref, rhs_ref, wide, hot_lo, hot_hi, low_sum, total):
    q = pl.program_id(0)
    groups, per, _ = rows_ref.shape
    faces = blocks_ref.shape[2]
    tiles = per // capacity - 1
    rows = tiles * LANES
    step = per + SKEW

    def gathered(at):
        pieces = [
            wide[pl.ds(at * capacity + c, groups, stride=step), :].astype(BF16) for c in range(capacity)
        ]
        return jnp.concatenate(pieces, axis=0)

    @pl.when(q == 0)
    def _():
        def widen(g, carry):
            wide[pl.ds(g * step, per), :] = rows_ref[g].astype(F32)
            return carry

        lax.fori_loop(0, groups, widen, 0, unroll=4)
        columns = lax.broadcasted_iota(jnp.int32, (groups, faces), 1)
        for c in range(capacity):
            hot_lo[c * groups:(c + 1) * groups, :] = (recv_ref[:, c:c + 1] == columns).astype(F32).astype(BF16)
            hot_hi[c * groups:(c + 1) * groups, :] = (
                (recv_ref[:, capacity + c:capacity + c + 1] == columns).astype(F32).astype(BF16)
            )
        low_sum[...] = lax.dot_general(gathered(tiles), hot_lo[...], TN, preferred_element_type=F32)

    @pl.when(q < tiles)
    def _():
        got = lax.dot_general(gathered(q), hot_hi[...], TN, preferred_element_type=F32)
        for f in range(faces // LANES):
            total[pl.ds(pl.multiple_of(f * rows + q * LANES, LANES), LANES), :] = got[:, f * LANES:(f + 1) * LANES]

    @pl.when(q == tiles - 1)
    def _():
        for m in range(NF_LO + 1):
            for f in range(faces // LANES):
                at = f * rows + (m if m < NF_LO else width) * width
                total[at:at + NF_LO, :] = (
                    total[at:at + NF_LO, :] + low_sum[m * NF_LO:(m + 1) * NF_LO, f * LANES:(f + 1) * LANES]
                )
        for f in range(faces // LANES):
            at = f * rows + width * width
            rhs_ref[:, f * LANES:(f + 1) * LANES] = total[at:at + width, :]

    @pl.when(q >= tiles)
    def _():
        for k in range(blocks_ref.shape[0]):
            i = (q - tiles) * blocks_ref.shape[0] + k
            for f in range(faces // LANES):
                blocks_ref[k, :, f * LANES:(f + 1) * LANES] = total[pl.ds(f * rows + i, width, stride=width), :]


def on_device(
    lo_ainv, lo_geom, lo_load, lo_degree, lo_send, hi_geom, hi_load, hi_degree, hi_slot, hi_ainv, hi_send,
    recv_face, lift_ref, trace_ref, face_mass,
):
    width = face_mass.shape[0]
    inner, _, elements = hi_ainv.shape
    groups = lax.axis_size("geo")
    capacity = 6 * lo_ainv.shape[2] // groups
    tiles = -(-width * (width + 1) // LANES)
    rows = tiles * LANES
    per = capacity * (tiles + 1)
    faces = groups * capacity

    record = pl.pallas_call(
        record_kernel,
        out_shape=jax.ShapeDtypeStruct((elements, LANES), F32),
        in_specs=[VMEM] * 4,
        out_specs=VMEM,
        name="record",
    )(hi_geom, hi_load, hi_degree[None, :], hi_slot[None, :])
    record = lax.all_to_all(record, "deg", split_axis=0, concat_axis=0, tiled=True)

    turned = jnp.transpose(trace_ref, (0, 2, 3, 1))

    def stacked(operator):
        wide = -(-operator.shape[3] // 8) * 8
        operator = jnp.pad(operator, ((0, 0), (0, 0), (0, 0), (0, wide - operator.shape[3])))
        return jnp.transpose(operator, (1, 2, 0, 3)).reshape(-1, TERMS * wide).astype(BF16)

    trace_hi = stacked(turned)
    trace_lo = stacked(turned[:, :, :NF_LO, :NI_LO])

    low_particular, placed = pl.pallas_call(
        functools.partial(low_kernel, capacity),
        out_shape=(
            jax.ShapeDtypeStruct((NI_LO, elements), F32),
            jax.ShapeDtypeStruct((groups * capacity, LANES), F32),
        ),
        in_specs=[VMEM] * 8,
        out_specs=(VMEM, VMEM),
        scratch_shapes=[
            pltpu.VMEM((4, TERMS * LO_PAD, NI_LO), BF16),
            pltpu.VMEM((NI_LO * 4 * NF_LO, LANES), F32),
            pltpu.VMEM((NI_LO, LANES), F32),
            pltpu.VMEM((NI_LO, LANES), F32),
            pltpu.VMEM((4 * LANES, LANES), F32),
            pltpu.VMEM((NF_LO, LO_PAD, LANES), F32),
            pltpu.VMEM((groups * capacity, 4 * LANES), BF16),
            pltpu.VMEM((LANES, 4 * LANES), BF16),
        ],
        cost_estimate=pl.CostEstimate(flops=400_000_000, bytes_accessed=2_000_000, transcendentals=0),
        name="low",
    )(lo_ainv, lo_geom, lo_load, lo_degree[None, :], lo_send, lift_ref, trace_lo, face_mass)

    high_particular, outgoing = pl.pallas_call(
        functools.partial(high_kernel, capacity),
        out_shape=(
            jax.ShapeDtypeStruct((inner, elements), F32),
            jax.ShapeDtypeStruct((groups, per, LANES), BF16),
        ),
        in_specs=[VMEM] * 7,
        out_specs=(VMEM, VMEM),
        scratch_shapes=[
            pltpu.VMEM((4, TERMS * HI_PAD, inner), BF16),
            pltpu.VMEM((inner * 4 * width, LANES), F32),
            pltpu.VMEM((inner, LANES), F32),
            pltpu.VMEM((inner, LANES), F32),
            pltpu.VMEM((4 * rows, LANES), F32),
            pltpu.VMEM((width, HI_PAD, LANES), F32),
            pltpu.VMEM((groups * capacity, 4 * LANES), BF16),
            pltpu.VMEM((2 * LANES, 4 * LANES), BF16),
            pltpu.VMEM((LANES, LANES), F32),
            pltpu.VMEM((groups * (per + SKEW), LANES), F32),
        ],
        compiler_params=pltpu.CompilerParams(vmem_limit_bytes=48 << 20),
        name="high",
    )(hi_ainv, record, hi_send, lift_ref, trace_hi, face_mass, placed)

    arrived = lax.all_to_all(outgoing, "geo", split_axis=0, concat_axis=0, tiled=True)

    plan = recv_face.reshape(groups, 2 * capacity)
    share = width // 7
    blocks, right = pl.pallas_call(
        functools.partial(accumulate_kernel, capacity, width),
        out_shape=(
            jax.ShapeDtypeStruct((width, width, faces), F32),
            jax.ShapeDtypeStruct((width, faces), F32),
        ),
        grid=(tiles + 7,),
        in_specs=[
            pl.BlockSpec((groups, per, LANES), lambda q: (0, 0, 0)),
            pl.BlockSpec((groups, 2 * capacity), lambda q: (0, 0)),
        ],
        out_specs=(
            pl.BlockSpec((share, width, faces), lambda q: (jnp.maximum(q - tiles, 0), 0, 0)),
            pl.BlockSpec((width, faces), lambda q: (0, 0)),
        ),
        scratch_shapes=[
            pltpu.VMEM((groups * (per + SKEW), LANES), F32),
            pltpu.VMEM((groups * capacity, faces), BF16),
            pltpu.VMEM((groups * capacity, faces), BF16),
            pltpu.VMEM((LANES, faces), F32),
            pltpu.VMEM((faces // LANES * rows, LANES), F32),
        ],
        compiler_params=pltpu.CompilerParams(vmem_limit_bytes=48 << 20),
        name="accumulate",
    )(arrived, plan)
    return (low_particular, high_particular, blocks, right)


def solution(mesh):
    both = ("geo", "deg")
    in_specs = (
        P(None, None, both), P(None, both), P(None, both), P(both), P(None, both), P(None, both), P(None, both),
        P(both), P(both), P(None, None, both), P(None, both), P(both), P(), P(), P(),
    )
    out_specs = (P(None, both), P(None, both), P(None, None, both), P(None, both))
    return jax.shard_map(on_device, mesh=mesh, in_specs=in_specs, out_specs=out_specs, check_vma=False)
```

```python
import functools

import jax
import jax.numpy as jnp
from jax import lax
from jax.experimental import pallas as pl
from jax.experimental.pallas import tpu as pltpu
from jax.sharding import PartitionSpec as P

F32 = jnp.float32
BF16 = jnp.bfloat16
LANES = 128
TERMS = 4
NF_LO = 10
NI_LO = 20
LO_PAD = 16
HI_PAD = 32
SKEW = 4
UNROLL = 2
UNROLL_C = 1
NT = (((1,), (1,)), ((), ()))
TN = (((0,), (0,)), ((), ()))
VMEM = pl.BlockSpec(memory_space=pltpu.VMEM)
ANY = pl.BlockSpec(memory_space=pl.ANY)
MESH = pl.DeviceIdType.MESH
LOW_ROWS = 8


def masks(degree, inner_width, face_width):
    inner_count = (degree + 1.0) * (degree + 2.0) * (degree + 3.0) / 6.0
    face_count = (degree + 1.0) * (degree + 2.0) / 2.0
    elements = degree.shape[1]
    inner_row = lax.broadcasted_iota(jnp.int32, (inner_width, elements), 0).astype(F32)
    face_row = lax.broadcasted_iota(jnp.int32, (face_width, elements), 0).astype(F32)
    inner_mask = (inner_row < inner_count).astype(F32)
    face_mask = (face_row < face_count).astype(F32)
    return inner_mask, face_mask


def condense_body(
    ainv_ref, geom, load, degree, lift_ref, trace_ref, mass_ref, part_ref,
    lmat, solved, masked, rhs_load, stack, massb, width, inner, pad, rows, between=None
):
    am = 4 * width
    depth = trace_ref.shape[1] // TERMS
    inner_mask, face_mask = masks(degree, inner, pad)
    masked[...] = inner_mask
    rhs_load[...] = load * inner_mask
    for t in range(TERMS):
        for a in range(4):
            piece = lift_ref[t, a][:width, :inner]
            piece = jnp.concatenate([piece, jnp.zeros((pad - width, inner), F32)], axis=0)
            for g in range(pad // 8):
                at = (g * TERMS + t) * 8
                lmat[a, at:at + 8, :] = piece[g * 8:(g + 1) * 8].astype(BF16)
    mass = mass_ref[...][:width, :width]
    mass = jnp.concatenate([mass, jnp.zeros((pad - width, width), F32)], axis=0)
    for m in range(width):
        massb[m] = jnp.broadcast_to(mass[:, m:m + 1], (pad, LANES))

    def combined(out, k, g, scales):
        total = None
        for t in range(TERMS):
            at = (g * TERMS + t) * 8
            term = out[at:at + 8, k * LANES:(k + 1) * LANES] * scales[t]
            total = term if total is None else total + term
        return total

    trace_g = [geom[TERMS + t:TERMS + t + 1, :] for t in range(TERMS)]

    filler = jnp.zeros((depth - inner, LANES), F32)

    def solve(pair, carry):
        columns = []
        for k in range(2):
            j = 2 * pair + k
            block = ainv_ref[j].astype(F32)
            row_mask = masked[pl.ds(j, 1), :]
            part_ref[pl.ds(j, 1), :] = row_mask * jnp.sum(block * rhs_load[...], axis=0, keepdims=True)
            block = block * masked[...]
            stacked = []
            for t in range(TERMS):
                stacked += [block * (trace_g[t] * row_mask), filler]
            columns.append(jnp.concatenate(stacked, axis=0).astype(BF16))
        out = jnp.dot(trace_ref[...], jnp.concatenate(columns, axis=1), preferred_element_type=F32)
        for k in range(2):
            solved[pl.ds(2 * pair + k, am, stride=inner), :] = out[:, k * LANES:(k + 1) * LANES]
        return carry

    lax.fori_loop(0, inner // 2, solve, 0, unroll=UNROLL)
    if between is not None:
        between()

    lift_g = [jnp.broadcast_to(geom[t:t + 1, :], (8, LANES)) for t in range(TERMS)]

    def mixed(out, k):
        return jnp.concatenate([combined(out, k, g, lift_g) for g in range(pad // 8)], axis=0)

    part = part_ref[...].astype(BF16)
    for a in range(4):
        out = jnp.dot(lmat[a], part, preferred_element_type=F32)
        value = -(mixed(out, 0) * face_mask)
        stack[a * rows + width * width:a * rows + width * width + width, :] = value[:width]
    scales = [geom[2 * TERMS + a:2 * TERMS + a + 1, :] for a in range(4)]

    def couple(pair, carry):
        for a in range(4):
            columns = []
            for k in range(2):
                m = 2 * pair + k
                columns.append(solved[pl.ds((a * width + m) * inner, inner), :].astype(BF16))
            out = jnp.dot(lmat[a], jnp.concatenate(columns, axis=1), preferred_element_type=F32)
            for k in range(2):
                m = 2 * pair + k
                column_mask = (m.astype(F32) < (degree + 1.0) * (degree + 2.0) / 2.0).astype(F32)
                value = (massb[m] * scales[a] - mixed(out, k)) * (face_mask * column_mask)
                stack[pl.ds(a * rows + m * width, width), :] = value[:width]
        return carry

    lax.fori_loop(0, width // 2, couple, 0, unroll=UNROLL_C)


def one_hots(send_ref, chosen, capacity):
    groups = chosen.shape[0] // capacity
    for a in range(4):
        positions = send_ref[a:a + 1, :]
        for c in range(capacity):
            want = lax.broadcasted_iota(jnp.int32, (groups, LANES), 0) * capacity + c
            chosen[c * groups:(c + 1) * groups, a * LANES:(a + 1) * LANES] = (
                (want == positions).astype(F32).astype(BF16)
            )


def record_kernel(geom_ref, load_ref, degree_ref, slot_ref, out_ref):
    count = geom_ref.shape[0] + load_ref.shape[0] + 1
    record = jnp.concatenate(
        [load_ref[...].astype(F32), geom_ref[...], degree_ref[...].astype(F32),
         jnp.zeros((LANES - count, LANES), F32)], axis=0
    )
    hot = (lax.broadcasted_iota(jnp.int32, (LANES, LANES), 0) == slot_ref[...]).astype(F32)
    out_ref[...] = lax.dot_general(hot, record, NT, precision=lax.Precision.HIGHEST, preferred_element_type=F32)


def low_kernel(
    capacity, ainv_ref, geom_ref, load_ref, degree_ref, send_ref, lift_ref, trace_ref, mass_ref,
    part_ref, out_ref, lmat, solved, masked, rhs_load, stack, massb, chosen, rowsb, wide
):
    groups = out_ref.shape[0]
    step = LOW_ROWS + SKEW
    stack[...] = jnp.zeros_like(stack)
    condense_body(
        ainv_ref, geom_ref[...], load_ref[...].astype(F32), degree_ref[...].astype(F32), lift_ref, trace_ref,
        mass_ref, part_ref, lmat, solved, masked, rhs_load, stack, massb,
        NF_LO, NI_LO, LO_PAD, LANES,
    )
    one_hots(send_ref, chosen, capacity)
    for a in range(4):
        rowsb[:, a * LANES:(a + 1) * LANES] = stack[a * LANES:(a + 1) * LANES, :].astype(BF16)
    got = lax.dot_general(chosen[...], rowsb[...], NT, preferred_element_type=F32)
    for c in range(capacity):
        wide[pl.ds(c, groups, stride=step), :] = got[c * groups:(c + 1) * groups, :]
    for c in range(capacity, LOW_ROWS):
        wide[pl.ds(c, groups, stride=step), :] = jnp.zeros((groups, LANES), F32)

    def narrow(o, carry):
        out_ref[o] = wide[pl.ds(o * step, LOW_ROWS), :].astype(BF16)
        return carry

    lax.fori_loop(0, groups, narrow, 0, unroll=4)


def peer_at(me, k, groups):
    j = lax.rem(k * 37, groups)
    side = 8 if groups % 16 == 0 else 1
    outer = groups // (2 * side)
    y = lax.rem(me // (2 * side) + j // (2 * side), outer)
    z = lax.rem(lax.rem(me // 2, side) + lax.rem(j // 2, side), side)
    core = lax.rem(me + j, 2)
    return (y * side + z) * 2 + core


def high_kernel(
    capacity, ainv_ref, record_ref, send_ref, lift_ref, trace_ref, mass_ref, low_ref,
    part_ref, rows_ref, low_rows_ref, lmat, solved, masked, rhs_load, stack, massb, chosen, rowsb, rec, wide, outgoing,
    send_sem, recv_sem, own_sem
):
    inner = ainv_ref.shape[0]
    width = mass_ref.shape[0]
    groups, per, _ = rows_ref.shape
    used = width * (width + 1)
    full = used // LANES
    tiles = full + 1
    rows = tiles * LANES
    step = per + SKEW
    half = LANES // 2
    me = lax.axis_index("geo")
    barrier = pltpu.get_barrier_semaphore()

    def greet(k, carry):
        pl.semaphore_signal(barrier, inc=1, device_id={"geo": peer_at(me, k, groups)}, device_id_type=MESH)
        return carry

    lax.fori_loop(1, groups, greet, 0)

    def send_all(source, target, at):
        def send(k, carry):
            peer = peer_at(me, k, groups)
            pltpu.make_async_remote_copy(
                src_ref=source.at[peer], dst_ref=target.at[me], send_sem=send_sem.at[at], recv_sem=recv_sem.at[at],
                device_id={"geo": peer}, device_id_type=MESH,
            ).start()
            return carry

        lax.fori_loop(1, groups, send, 0)
        pltpu.make_async_copy(source.at[me], target.at[me], own_sem.at[at]).start()

    def wait_all(source, target, at):
        pltpu.make_async_copy(source.at[me], target.at[me], own_sem.at[at]).wait()
        sent = source.at[pl.ds(0, groups - 1)]
        pltpu.make_async_copy(sent, sent, send_sem.at[at]).wait()
        come = target.at[pl.ds(0, groups - 1)]
        pltpu.make_async_copy(come, come, recv_sem.at[at]).wait()

    def between():
        pl.semaphore_wait(barrier, groups - 1)
        send_all(low_ref, low_rows_ref, 0)

    rec[...] = record_ref[...].T
    geom = rec[inner:inner + 12, :]
    degree = rec[inner + 12:inner + 13, :]
    for a in range(4):
        stack[a * rows + used:(a + 1) * rows, :] = jnp.zeros((rows - used, LANES), F32)
    condense_body(
        ainv_ref, geom, rec[:inner, :], degree, lift_ref, trace_ref, mass_ref, part_ref,
        lmat, solved, masked, rhs_load, stack, massb,
        width, inner, HI_PAD, rows, between,
    )
    one_hots(send_ref, chosen, capacity)

    def placed(q, count):
        for k in range(count):
            for a in range(4):
                piece = stack[pl.ds(pl.multiple_of(a * rows + (q + k) * LANES, LANES), LANES), :]
                rowsb[k * LANES:(k + 1) * LANES, a * LANES:(a + 1) * LANES] = piece.astype(BF16)
        return lax.dot_general(chosen[...], rowsb[:count * LANES], NT, preferred_element_type=F32)

    def place_pair(pair, carry):
        got = placed(2 * pair, 2)
        for k in range(2):
            for c in range(capacity):
                wide[pl.ds((2 * pair + k) * capacity + c, groups, stride=step), :] = (
                    got[c * groups:(c + 1) * groups, k * LANES:(k + 1) * LANES]
                )
        return carry

    lax.fori_loop(0, full // 2, place_pair, 0)
    tail = placed(full, 1)
    for c in range(0, capacity, 2):
        even = tail[c * groups:(c + 1) * groups, :]
        odd = tail[(c + 1) * groups:(c + 2) * groups, :]
        wide[pl.ds(full * capacity + c // 2, groups, stride=step), :] = even + pltpu.roll(odd, half, axis=1)
    for r in range(full * capacity + capacity // 2, per):
        wide[pl.ds(r, groups, stride=step), :] = jnp.zeros((groups, LANES), F32)

    def narrow(o, carry):
        outgoing[o] = wide[pl.ds(o * step, per), :].astype(BF16)
        return carry

    lax.fori_loop(0, groups, narrow, 0, unroll=4)
    send_all(outgoing, rows_ref, 1)
    wait_all(low_ref, low_rows_ref, 0)
    wait_all(outgoing, rows_ref, 1)


def accumulate_kernel(
    capacity, width, rows_ref, low_ref, recv_ref, blocks_ref, rhs_ref, wide, low_wide, hot_lo, hot_hi, low_sum, total
):
    q = pl.program_id(0)
    groups, per, _ = rows_ref.shape
    faces = blocks_ref.shape[2]
    full = width * (width + 1) // LANES
    tiles = full + 1
    rows = tiles * LANES
    step = per + SKEW
    low_step = LOW_ROWS + SKEW

    def gathered(at):
        pieces = [
            wide[pl.ds(at * capacity + c, groups, stride=step), :].astype(BF16) for c in range(capacity)
        ]
        return jnp.concatenate(pieces, axis=0)

    def tails():
        pieces = []
        for c in range(capacity):
            piece = wide[pl.ds(full * capacity + c // 2, groups, stride=step), :]
            pieces.append((pltpu.roll(piece, LANES // 2, axis=1) if c % 2 else piece).astype(BF16))
        return jnp.concatenate(pieces, axis=0)

    def lows():
        pieces = [low_wide[pl.ds(c, groups, stride=low_step), :].astype(BF16) for c in range(capacity)]
        return jnp.concatenate(pieces, axis=0)

    @pl.when(q == 0)
    def _():
        def widen(g, carry):
            wide[pl.ds(g * step, per), :] = rows_ref[g].astype(F32)
            low_wide[pl.ds(g * low_step, LOW_ROWS), :] = low_ref[g].astype(F32)
            return carry

        lax.fori_loop(0, groups, widen, 0, unroll=4)
        columns = lax.broadcasted_iota(jnp.int32, (groups, faces), 1)
        for c in range(capacity):
            hot_lo[c * groups:(c + 1) * groups, :] = (recv_ref[:, c:c + 1] == columns).astype(F32).astype(BF16)
            hot_hi[c * groups:(c + 1) * groups, :] = (
                (recv_ref[:, capacity + c:capacity + c + 1] == columns).astype(F32).astype(BF16)
            )
        low_sum[...] = lax.dot_general(lows(), hot_lo[...], TN, preferred_element_type=F32)

    def add(pieces):
        got = lax.dot_general(pieces, hot_hi[...], TN, preferred_element_type=F32)
        for f in range(faces // LANES):
            total[pl.ds(pl.multiple_of(f * rows + q * LANES, LANES), LANES), :] = got[:, f * LANES:(f + 1) * LANES]

    @pl.when(q < full)
    def _():
        add(gathered(q))

    @pl.when(q == full)
    def _():
        add(tails())
        for m in range(NF_LO + 1):
            for f in range(faces // LANES):
                at = f * rows + (m if m < NF_LO else width) * width
                total[at:at + NF_LO, :] = (
                    total[at:at + NF_LO, :] + low_sum[m * NF_LO:(m + 1) * NF_LO, f * LANES:(f + 1) * LANES]
                )
        for f in range(faces // LANES):
            at = f * rows + width * width
            rhs_ref[:, f * LANES:(f + 1) * LANES] = total[at:at + width, :]

    @pl.when(q >= tiles)
    def _():
        for k in range(blocks_ref.shape[0]):
            i = (q - tiles) * blocks_ref.shape[0] + k
            for f in range(faces // LANES):
                blocks_ref[k, :, f * LANES:(f + 1) * LANES] = total[pl.ds(f * rows + i, width, stride=width), :]


def on_device(
    lo_ainv, lo_geom, lo_load, lo_degree, lo_send, hi_geom, hi_load, hi_degree, hi_slot, hi_ainv, hi_send,
    recv_face, lift_ref, trace_ref, face_mass,
):
    width = face_mass.shape[0]
    inner, _, elements = hi_ainv.shape
    groups = lax.axis_size("geo")
    capacity = 6 * lo_ainv.shape[2] // groups
    full = width * (width + 1) // LANES
    tiles = full + 1
    rows = tiles * LANES
    per = -(-(capacity * full + capacity // 2) // 8) * 8
    faces = groups * capacity

    record = pl.pallas_call(
        record_kernel,
        out_shape=jax.ShapeDtypeStruct((elements, LANES), F32),
        in_specs=[VMEM] * 4,
        out_specs=VMEM,
        name="record",
    )(hi_geom, hi_load, hi_degree[None, :], hi_slot[None, :])
    record = lax.all_to_all(record, "deg", split_axis=0, concat_axis=0, tiled=True)

    turned = jnp.transpose(trace_ref, (0, 2, 3, 1))

    def stacked(operator):
        wide = -(-operator.shape[3] // 8) * 8
        operator = jnp.pad(operator, ((0, 0), (0, 0), (0, 0), (0, wide - operator.shape[3])))
        return jnp.transpose(operator, (1, 2, 0, 3)).reshape(-1, TERMS * wide).astype(BF16)

    trace_hi = stacked(turned)
    trace_lo = stacked(turned[:, :, :NF_LO, :NI_LO])

    low_particular, placed = pl.pallas_call(
        functools.partial(low_kernel, capacity),
        out_shape=(
            jax.ShapeDtypeStruct((NI_LO, elements), F32),
            jax.ShapeDtypeStruct((groups, LOW_ROWS, LANES), BF16),
        ),
        in_specs=[VMEM] * 8,
        out_specs=(VMEM, VMEM),
        scratch_shapes=[
            pltpu.VMEM((4, TERMS * LO_PAD, NI_LO), BF16),
            pltpu.VMEM((NI_LO * 4 * NF_LO, LANES), F32),
            pltpu.VMEM((NI_LO, LANES), F32),
            pltpu.VMEM((NI_LO, LANES), F32),
            pltpu.VMEM((4 * LANES, LANES), F32),
            pltpu.VMEM((NF_LO, LO_PAD, LANES), F32),
            pltpu.VMEM((groups * capacity, 4 * LANES), BF16),
            pltpu.VMEM((LANES, 4 * LANES), BF16),
            pltpu.VMEM((groups * (LOW_ROWS + SKEW), LANES), F32),
        ],
        cost_estimate=pl.CostEstimate(flops=400_000_000, bytes_accessed=2_000_000, transcendentals=0),
        name="low",
    )(lo_ainv, lo_geom, lo_load, lo_degree[None, :], lo_send, lift_ref, trace_lo, face_mass)

    high_particular, arrived, low_arrived = pl.pallas_call(
        functools.partial(high_kernel, capacity),
        out_shape=(
            jax.ShapeDtypeStruct((inner, elements), F32),
            jax.ShapeDtypeStruct((groups, per, LANES), BF16),
            jax.ShapeDtypeStruct((groups, LOW_ROWS, LANES), BF16),
        ),
        in_specs=[VMEM] * 6 + [ANY],
        out_specs=(VMEM, ANY, ANY),
        scratch_shapes=[
            pltpu.VMEM((4, TERMS * HI_PAD, inner), BF16),
            pltpu.VMEM((inner * 4 * width, LANES), F32),
            pltpu.VMEM((inner, LANES), F32),
            pltpu.VMEM((inner, LANES), F32),
            pltpu.VMEM((4 * rows, LANES), F32),
            pltpu.VMEM((width, HI_PAD, LANES), F32),
            pltpu.VMEM((groups * capacity, 4 * LANES), BF16),
            pltpu.VMEM((2 * LANES, 4 * LANES), BF16),
            pltpu.VMEM((LANES, LANES), F32),
            pltpu.VMEM((groups * (per + SKEW), LANES), F32),
            pltpu.VMEM((groups, per, LANES), BF16),
            pltpu.SemaphoreType.DMA((2,)),
            pltpu.SemaphoreType.DMA((2,)),
            pltpu.SemaphoreType.DMA((2,)),
        ],
        compiler_params=pltpu.CompilerParams(vmem_limit_bytes=40 << 20, collective_id=0, has_side_effects=True),
        name="high",
    )(hi_ainv, record, hi_send, lift_ref, trace_hi, face_mass, placed)

    plan = recv_face.reshape(groups, 2 * capacity)
    share = width // 7
    blocks, right = pl.pallas_call(
        functools.partial(accumulate_kernel, capacity, width),
        out_shape=(
            jax.ShapeDtypeStruct((width, width, faces), F32),
            jax.ShapeDtypeStruct((width, faces), F32),
        ),
        grid=(tiles + 7,),
        in_specs=[
            pl.BlockSpec((groups, per, LANES), lambda q: (0, 0, 0)),
            pl.BlockSpec((groups, LOW_ROWS, LANES), lambda q: (0, 0, 0)),
            pl.BlockSpec((groups, 2 * capacity), lambda q: (0, 0)),
        ],
        out_specs=(
            pl.BlockSpec((share, width, faces), lambda q: (jnp.maximum(q - tiles, 0), 0, 0)),
            pl.BlockSpec((width, faces), lambda q: (0, 0)),
        ),
        scratch_shapes=[
            pltpu.VMEM((groups * (per + SKEW), LANES), F32),
            pltpu.VMEM((groups * (LOW_ROWS + SKEW), LANES), F32),
            pltpu.VMEM((groups * capacity, faces), BF16),
            pltpu.VMEM((groups * capacity, faces), BF16),
            pltpu.VMEM((LANES, faces), F32),
            pltpu.VMEM((faces // LANES * rows, LANES), F32),
        ],
        compiler_params=pltpu.CompilerParams(vmem_limit_bytes=48 << 20),
        name="accumulate",
    )(arrived, low_arrived, plan)
    return (low_particular, high_particular, blocks, right)


def solution(mesh):
    both = ("geo", "deg")
    in_specs = (
        P(None, None, both), P(None, both), P(None, both), P(both), P(None, both), P(None, both), P(None, both),
        P(both), P(both), P(None, None, both), P(None, both), P(both), P(), P(), P(),
    )
    out_specs = (P(None, both), P(None, both), P(None, None, both), P(None, both))
    return jax.shard_map(on_device, mesh=mesh, in_specs=in_specs, out_specs=out_specs, check_vma=False)
```
